32 devices in a mesh: group: 2 (over x), atom: 16 (over z, y, core).
Axes of the slice: x: 2, y: 2, z: 4, core: 2. Of those that a mesh axis runs over, the one named last changes fastest.
Arguments:
- features: bfloat16 [8192, 128], P(('group', 'atom')), parts along dimension 0, may hold values from -6 to 6
- species: int32 [8192], P(('group', 'atom')), parts along dimension 0, may hold values from 0 to 88
- positions: float32 [3, 8192], P(None, ('group', 'atom')), parts along dimension 1, may hold values from 0 to 1
- miller: int32 [3, 8192], replicated, may hold values from -13 to 13, as said below
- species_table: bfloat16 [89, 128], replicated, may hold values from -3 to 3
- w_query: bfloat16 [2, 128, 128], replicated, may hold values from -0.5 to 0.5
- w_key: bfloat16 [2, 256, 128], replicated, may hold values from -0.375 to 0.375
- w_value: bfloat16 [2, 128, 128], replicated, may hold values from -0.5 to 0.5
- w_out: bfloat16 [2, 128, 128], replicated, may hold values from -0.5 to 0.5
- temper: float32 [2, 8], replicated, may hold values from 1 to 4
Outputs:
- refined: bfloat16 [8192, 128], P(('group', 'atom')), parts along dimension 0
The draws below stay inside these ranges and needn't reach their ends.
There are 2 independent parts, one for each index of `group`. The reference program is written for one: setup_inputs(seed, part) draws one part's arguments, and reference() takes and returns one part's arrays. A program takes and returns all parts, laid end to end along the dimension named above; an argument that names none is the same for every part. Nothing has to cross between parts.
Inputs may be any that keep to these rules, and one draw needn't show every extreme that they name: `miller`: the k-vectors are distinct and nonzero, one of each pair m and -m (the one whose first nonzero index is positive), each index within -13 to 13, both ends reached; columns are ordered by non-decreasing |m|^2, and every lattice vector with indices within -13 to 13 of smaller |m|^2 than the last column's in that half-space is present.
All inputs are finite; a program needn't handle non-finite values.
Results may differ from the reference program's by a relative error of at most 0.012.
Values may be sent and summed in bfloat16 or wider, within the bound.
No kernel may reach another device: no remote copies, remote signals or barrier semaphores. Data moves between devices by JAX's collectives and lax.ppermute only.
A program may use at most 128 MiB of HBM per device.

```python
import math
import jax
import jax.numpy as jnp
from jax import lax

KVECS = 8192
CHANNELS = 128
HEADS = 8
HDIM = 16
NSPEC = 89
LAYERS = 2
MILLER_MAX = 13
KEY_WIDTH = 128
ATOMS = 4096


def draw_miller(key, part):
    span = 2 * MILLER_MAX + 1
    cube = span * span * span
    flat = jnp.arange(cube, dtype=jnp.int32)
    index_x = flat // (span * span) - MILLER_MAX
    index_y = flat // span % span - MILLER_MAX
    index_z = flat % span - MILLER_MAX
    upper = (index_x > 0) | (index_x == 0) & (index_y > 0) | (index_x == 0) & (index_y == 0) & (index_z > 0)
    length_sq = index_x * index_x + index_y * index_y + index_z * index_z
    tiebreak = jax.random.permutation(key, cube).astype(jnp.int32)
    score = jnp.where(upper, length_sq * 65536 + tiebreak, 1073741824 + tiebreak)
    order_index = jnp.argsort(score, stable=True)[:KVECS]
    return jnp.stack([index_x, index_y, index_z])[:, order_index]


def touch_ends(array, stream_key, smallest, largest):
    dims = array.shape
    index_at = [jax.random.randint(jax.random.fold_in(stream_key, axis), (), 0, dims[axis]) for axis in range(len(dims))]
    array = array.at[tuple(index_at)].set(smallest)
    longest = dims.index(max(dims))
    index_at[longest] = (index_at[longest] + 1) % dims[longest]
    return array.at[tuple(index_at)].set(largest)


def block_scale(stream_key, shape, shards, least, largest):
    gain = 1.0
    for dim, blocks in shards:
        heights = jax.random.uniform(jax.random.fold_in(jax.random.fold_in(stream_key, 6), dim), (blocks,), jnp.float32, least / len(shards), largest / len(shards))
        gain = gain * jnp.repeat(jnp.exp(heights), shape[dim] // blocks).reshape((-1,) + (1,) * (len(shape) - 1 - dim))
    return gain


def bell_draw(own_key, dims, scale, reach, pieces=(), kind=jnp.bfloat16):
    gain = block_scale(own_key, dims, pieces, -0.22, 0.18) if pieces else 1.0
    array = jax.random.normal(own_key, dims, jnp.float32) * scale * gain
    return jnp.minimum(jnp.maximum(array, -reach), reach).astype(kind)


def setup_inputs(seed: int = 0, part: int = 0) -> dict:
    key_of = jax.random.split(jax.random.key(seed), 11)
    part_keys = jax.random.split(jax.random.fold_in(key_of[10], part), 11)
    features = bell_draw(part_keys[0], (ATOMS, CHANNELS), 1.0, 6.0, ((0, 16),))
    species = touch_ends(jax.random.randint(part_keys[1], (ATOMS,), 0, NSPEC), jax.random.fold_in(part_keys[1], 1), 0, NSPEC - 1).astype(jnp.int32)
    positions = jnp.clip(1.0 * jax.random.uniform(part_keys[2], (3, ATOMS), jnp.float32) ** block_scale(part_keys[2], (3, ATOMS), ((1, 16),), -0.2, 0.2), 0.0, 1.0)
    miller = draw_miller(jax.random.fold_in(key_of[10], 71), part)
    species_table = bell_draw(key_of[4], (NSPEC, CHANNELS), 0.5, 3.0)
    w_query = bell_draw(key_of[5], (LAYERS, CHANNELS, KEY_WIDTH), CHANNELS ** -0.5, 0.5)
    w_key = bell_draw(key_of[6], (LAYERS, 2 * CHANNELS, KEY_WIDTH), (2 * CHANNELS) ** -0.5, 0.375)
    w_value = bell_draw(key_of[7], (LAYERS, CHANNELS, KEY_WIDTH), CHANNELS ** -0.5, 0.5)
    w_out = bell_draw(key_of[8], (LAYERS, KEY_WIDTH, CHANNELS), KEY_WIDTH ** -0.5, 0.5)
    temper = jnp.clip(jnp.exp(jax.random.uniform(key_of[9], (LAYERS, HEADS), jnp.float32, math.log(1.0), math.log(4.0))), 1.0, 4.0)
    return {"features": features, "species": species, "positions": positions, "miller": miller, "species_table": species_table, "w_query": w_query, "w_key": w_key, "w_value": w_value, "w_out": w_out, "temper": temper}


DAMP = 0.005
EPS = 1e-06
POWER_EPS = 1e-05

def angles(miller, positions):
    mfloat = miller.astype(jnp.float32)
    turns = mfloat[0][:, None] * positions[0][None, :] + mfloat[1][:, None] * positions[1][None, :]
    turns = turns + mfloat[2][:, None] * positions[2][None, :]
    return 2.0 * math.pi * turns

def damping(miller):
    mfloat = miller.astype(jnp.float32)
    return jnp.exp(-DAMP * (mfloat[0] * mfloat[0] + mfloat[1] * mfloat[1] + mfloat[2] * mfloat[2]))

def phase_product(miller, positions, atom_rows):
    theta = angles(miller, positions)
    real_part = jnp.dot(jnp.cos(theta).astype(jnp.bfloat16), atom_rows, preferred_element_type=jnp.float32)
    imag_part = jnp.dot(jnp.sin(theta).astype(jnp.bfloat16), atom_rows, preferred_element_type=jnp.float32)
    return jnp.concatenate([real_part, imag_part], axis=1)

def rms_scale(values):
    return values * lax.rsqrt(lax.optimization_barrier(jnp.mean(values * values, axis=-1, keepdims=True)) + EPS)

def reference(features, species, positions, miller, species_table, w_query, w_key, w_value, w_out, temper):
    levels = jnp.arange(NSPEC, dtype=jnp.int32)
    onehot = (species[:, None] == levels[None, :]).astype(jnp.bfloat16)
    hidden = (features.astype(jnp.float32) + jnp.dot(onehot, species_table, preferred_element_type=jnp.float32)).astype(jnp.bfloat16)
    atom_block = min(256, ATOMS)
    k_block = min(512, KVECS)
    miller_blocks = miller.reshape(3, KVECS // k_block, k_block).transpose(1, 0, 2)
    position_blocks = positions.reshape(3, ATOMS // atom_block, atom_block).transpose(1, 0, 2)
    for layer_index in range(LAYERS):

        def factor_block(miller_part):
            return phase_product(miller_part, positions, hidden) * (damping(miller_part) / math.sqrt(ATOMS))[:, None]
        factor = lax.map(factor_block, miller_blocks).reshape(KVECS, 2 * CHANNELS)
        factor_b = factor.astype(jnp.bfloat16)
        fac_wide = factor_b.astype(jnp.float32)
        power_sum = lax.optimization_barrier(jnp.sum(fac_wide[:, :CHANNELS] * fac_wide[:, :CHANNELS] + fac_wide[:, CHANNELS:] * fac_wide[:, CHANNELS:], axis=0))
        power_scale = lax.rsqrt(power_sum / KVECS + POWER_EPS)
        both_scale = jnp.concatenate([power_scale, power_scale])
        key_scaled = (both_scale[:, None] * w_key[layer_index].astype(jnp.float32)).astype(jnp.bfloat16)
        value_scaled = (power_scale[:, None] * w_value[layer_index].astype(jnp.float32)).astype(jnp.bfloat16)
        key_rows = rms_scale(jnp.dot(factor_b, key_scaled, preferred_element_type=jnp.float32)).astype(jnp.bfloat16)
        value_real = jnp.dot(factor_b[:, :CHANNELS], value_scaled, preferred_element_type=jnp.float32).astype(jnp.bfloat16)
        value_imag = jnp.dot(factor_b[:, CHANNELS:], value_scaled, preferred_element_type=jnp.float32).astype(jnp.bfloat16)
        queries = rms_scale(jnp.dot(hidden, w_query[layer_index], preferred_element_type=jnp.float32)).astype(jnp.bfloat16)
        query_blocks = queries.reshape(ATOMS // atom_block, atom_block, KEY_WIDTH)
        temp_scale = temper[layer_index] / 16.0
        keys_wide = key_rows.astype(jnp.float32).reshape(KVECS, HEADS, HDIM)
        real_wide = value_real.astype(jnp.float32).reshape(KVECS, HEADS, HDIM)
        imag_wide = value_imag.astype(jnp.float32).reshape(KVECS, HEADS, HDIM)

        def attend_block(operands):
            query_part, position_part = operands
            query_wide = query_part.astype(jnp.float32).reshape(atom_block, HEADS, HDIM)
            scores = jnp.einsum('ahd,khd->ahk', query_wide, keys_wide)
            weights = jnp.exp(scores * temp_scale[None, :, None])
            theta = angles(miller, position_part).T
            weight_cos = (weights * jnp.cos(theta)[:, None, :]).astype(jnp.bfloat16)
            weight_sin = (weights * jnp.sin(theta)[:, None, :]).astype(jnp.bfloat16)
            numerator = jnp.einsum('ahk,khd->ahd', weight_cos.astype(jnp.float32), real_wide) + jnp.einsum('ahk,khd->ahd', weight_sin.astype(jnp.float32), imag_wide)
            totals = lax.optimization_barrier(jnp.sum(weights, axis=2))
            return (numerator / totals[:, :, None]).reshape(atom_block, KEY_WIDTH)
        mixed = lax.map(attend_block, (query_blocks, position_blocks)).reshape(ATOMS, KEY_WIDTH)
        normed = rms_scale(mixed).astype(jnp.bfloat16)
        hidden = (hidden.astype(jnp.float32) + jnp.dot(normed, w_out[layer_index], preferred_element_type=jnp.float32)).astype(jnp.bfloat16)
    return hidden
```

```python
import functools
import math

import jax
import jax.numpy as jnp
import numpy as np
from jax import lax
from jax.experimental import pallas as pl
from jax.experimental.pallas import tpu as pltpu
from jax.sharding import PartitionSpec as P

DAMP = 0.005
EPS = 1e-06
POWER_EPS = 1e-05
MILLER_MAX = 13
ROW_TILE = 16
SUB_ROWS = 256
NEVER = -30000.0
F32 = jnp.float32
BF16 = jnp.bfloat16
NT = (((1,), (1,)), ((), ()))


class Lattice:
    def __init__(self, kvecs):
        top = MILLER_MAX
        side = np.arange(-top, top + 1)
        gx, gy, gz = np.meshgrid(side, side, side, indexing="ij")
        upper = (gx > 0) | ((gx == 0) & (gy > 0)) | ((gx == 0) & (gy == 0) & (gz > 0))
        lengths = np.sort((gx * gx + gy * gy + gz * gz)[upper])
        self.radius = int(lengths[kvecs - 1])
        self.inner = int((lengths < self.radius).sum())
        pairs = [(x, y) for x in range(top + 1) for y in range(-top, top + 1) if x > 0 or y >= 0]
        pairs.sort(key=lambda p: p[0] ** 2 + p[1] ** 2)
        count = -(-len(pairs) // ROW_TILE) * ROW_TILE
        self.pair_rows = count
        self.px = np.array([p[0] for p in pairs] + [0] * (count - len(pairs)), np.int32)
        self.py = np.array([p[1] for p in pairs] + [0] * (count - len(pairs)), np.int32)
        real = np.arange(count) < len(pairs)
        flat = self.px**2 + self.py**2
        self.planes = []
        self.heights = []
        offset = 0
        row_code, row_len = [], []
        self.levels = 2 * top + 1
        self.tab_len = np.full((count, self.levels), self.radius + 1, np.int32)
        self.tab_code = np.full((count, self.levels), -1, np.int32)
        for level in range(top + 1):
            inside = real & (flat + level * level <= self.radius)
            height = -(-int(inside.sum()) // ROW_TILE) * ROW_TILE
            self.heights.append(height)
            offsets = []
            for sign in (1, -1) if level else (1,):
                mz = sign * level
                keep = inside & ((self.px > 0) | (self.py > 0) | (mz > 0))
                length = np.where(keep, flat + mz * mz, self.radius + 1)
                code = np.where(keep, self.code(self.px, self.py, mz), -1)
                column = 2 * level - (sign > 0) if level else 0
                self.tab_len[:, column] = length
                self.tab_code[:, column] = code
                row_len.append(length[:height])
                row_code.append(code[:height])
                offsets.append((offset, column))
                offset += height
            self.planes.append(offsets)
        rows = -(-offset // SUB_ROWS) * SUB_ROWS
        self.rows = rows
        self.row_len = np.concatenate(row_len + [np.full(rows - offset, self.radius + 1)]).astype(np.int32)
        self.row_code = np.concatenate(row_code + [np.full(rows - offset, -1)]).astype(np.int32)
        self.used = offset

    @staticmethod
    def code(x, y, z):
        return ((x + 16) * 32 + (y + 16)) * 32 + (z + 16)


def fit_half_turn():
    nodes = 0.25 * (1 + np.cos(np.pi * (np.arange(64) + 0.5) / 64))
    square = nodes * nodes
    sine = np.polynomial.polynomial.polyfit(square, np.sin(np.pi * nodes) / nodes, 4)
    cosine = np.polynomial.polynomial.polyfit(square, np.cos(np.pi * nodes), 4)
    return [float(v) for v in sine], [float(v) for v in cosine]


SINE, COSINE = fit_half_turn()


def horner(coefs, u):
    total = jnp.full_like(u, coefs[-1])
    for c in coefs[-2::-1]:
        total = total * u + c
    return total


def cos_sin_turns(turns):
    part = turns - jnp.floor(turns + 0.5)
    u = part * part
    half_sin = part * horner(SINE, u)
    half_cos = horner(COSINE, u)
    return 1.0 - 2.0 * half_sin * half_sin, 2.0 * half_sin * half_cos


def vmem():
    return pl.BlockSpec(memory_space=pltpu.VMEM)


def pair_kernel(pair_ref, pos_ref, cos_ref, sin_ref):
    turns = pair_ref[:, 0:1] * pos_ref[0:1, :] + pair_ref[:, 1:2] * pos_ref[1:2, :]
    c, s = cos_sin_turns(turns)
    cos_ref[0] = c.astype(BF16)
    sin_ref[0] = s.astype(BF16)


def pair_tables(pair_cols, pos, chunk):
    rows, atoms = pair_cols.shape[0], pos.shape[1]
    out = jax.ShapeDtypeStruct((atoms // chunk, rows, chunk), BF16)
    spec = pl.BlockSpec((1, rows, chunk), lambda i: (i, 0, 0))
    return pl.pallas_call(
        pair_kernel,
        grid=(atoms // chunk,),
        in_specs=[
            pl.BlockSpec(pair_cols.shape, lambda i: (0, 0)),
            pl.BlockSpec((pos.shape[0], chunk), lambda i: (0, i)),
        ],
        out_specs=[spec, spec],
        out_shape=[out, out],
        name="pair_tables",
    )(pair_cols, pos)


def local_kernel(lat, pair_ref, pos_ref, cos_ref, sin_ref, c_buf, s_buf):
    turns = pair_ref[:, 0:1] * pos_ref[0:1, :] + pair_ref[:, 1:2] * pos_ref[1:2, :]
    c, s = cos_sin_turns(turns)
    c_buf[...] = c
    s_buf[...] = s
    for level, (height, offsets) in enumerate(zip(lat.heights, lat.planes)):
        cz, sz = cos_sin_turns(float(level) * pos_ref[2:3, :])
        c1, s1 = c_buf[:height, :], s_buf[:height, :]
        cc, ss, sc, cs = c1 * cz, s1 * sz, s1 * cz, c1 * sz
        for (offset, _), values in zip(offsets, ((cc - ss, sc + cs), (cc + ss, sc - cs))):
            cos_ref[offset : offset + height, :] = values[0].astype(BF16)
            sin_ref[offset : offset + height, :] = values[1].astype(BF16)
    if lat.rows > lat.used:
        blank = jnp.zeros((lat.rows - lat.used, cos_ref.shape[1]), BF16)
        cos_ref[lat.used :, :] = blank
        sin_ref[lat.used :, :] = blank


def local_tables(lat, pair_cols, pos):
    atoms = pos.shape[1]
    out = jax.ShapeDtypeStruct((lat.rows, atoms), BF16)
    return pl.pallas_call(
        functools.partial(local_kernel, lat),
        in_specs=[vmem()] * 2,
        out_specs=[vmem()] * 2,
        out_shape=[out, out],
        scratch_shapes=[pltpu.VMEM((lat.pair_rows, atoms), F32)] * 2,
        name="local_tables",
    )(pair_cols, pos)


def factor_kernel(lat, h_ref, z_ref, pc_ref, ps_ref, damp_ref, f_ref, pow_ref, acc):
    chunks, _, width = h_ref.shape
    pad = lat.pair_rows
    total = jnp.zeros((8, 2 * width), F32)
    for level, (height, offsets) in enumerate(zip(lat.heights, lat.planes)):
        acc[0:height, :] = jnp.zeros((height, 2 * width), F32)
        acc[pad : pad + height, :] = jnp.zeros((height, 2 * width), F32)

        def step(index, carry):
            h = h_ref[index].astype(F32)
            hc = (h * z_ref[index, :, level : level + 1]).astype(BF16)
            hs = (h * z_ref[index, :, 16 + level : 17 + level]).astype(BF16)
            rhs = jnp.concatenate([hc, hs], axis=1)
            acc[0:height, :] += jnp.dot(pc_ref[index, :height, :], rhs, preferred_element_type=F32)
            acc[pad : pad + height, :] += jnp.dot(
                ps_ref[index, :height, :], rhs, preferred_element_type=F32
            )
            return carry

        lax.fori_loop(0, chunks, step, 0)
        cc, cs = acc[0:height, :width], acc[0:height, width:]
        sc, ss = acc[pad : pad + height, :width], acc[pad : pad + height, width:]
        for (offset, column), (real, imag) in zip(offsets, ((cc - ss, sc + cs), (cc + ss, sc - cs))):
            damp = damp_ref[:height, column : column + 1]
            value = jnp.concatenate([real * damp, imag * damp], axis=1).astype(BF16)
            f_ref[offset : offset + height, :] = value
            wide = value.astype(F32)
            total = total + jnp.sum((wide * wide).reshape(height // 8, 8, 2 * width), axis=0)
    if lat.rows > lat.used:
        f_ref[lat.used :, :] = jnp.zeros((lat.rows - lat.used, 2 * width), BF16)
    pow_ref[...] = total


def factors(lat, hidden, z_cols, pair_cos, pair_sin, damp):
    chunks, _, chunk = pair_cos.shape
    width = hidden.shape[1]
    return pl.pallas_call(
        functools.partial(factor_kernel, lat),
        in_specs=[vmem()] * 5,
        out_specs=[vmem()] * 2,
        out_shape=[
            jax.ShapeDtypeStruct((lat.rows, 2 * width), BF16),
            jax.ShapeDtypeStruct((8, 2 * width), F32),
        ],
        scratch_shapes=[pltpu.VMEM((2 * lat.pair_rows, 2 * width), F32)],
        name="factors",
    )(
        hidden.reshape(chunks, chunk, width),
        z_cols.reshape(chunks, chunk, z_cols.shape[1]),
        pair_cos,
        pair_sin,
        damp,
    )


def attend_kernel(heads, f_ref, ks_ref, vs_ref, q_ref, b_ref, c_ref, s_ref, o_ref, t_ref):
    @pl.when(pl.program_id(0) == 0)
    def _():
        o_ref[...] = jnp.zeros_like(o_ref)
        t_ref[...] = jnp.zeros_like(t_ref)

    depth = o_ref.shape[0] // heads
    sub = SUB_ROWS
    for j in range(f_ref.shape[0] // sub):
        span = slice(j * sub, (j + 1) * sub)
        f = f_ref[span, :]
        width = f.shape[1] // 2
        key = jnp.dot(f, ks_ref[...], preferred_element_type=F32)
        key = (key * lax.rsqrt(jnp.mean(key * key, axis=-1, keepdims=True) + EPS)).astype(BF16)
        key = jnp.concatenate([key, b_ref[span, :]], axis=1)
        vr = lax.dot_general(vs_ref[...], f[:, :width], NT, preferred_element_type=F32).astype(BF16)
        vi = lax.dot_general(vs_ref[...], f[:, width:], NT, preferred_element_type=F32).astype(BF16)
        cos, sin = c_ref[span, :], s_ref[span, :]
        for h in range(heads):
            score = jnp.dot(key, q_ref[h], preferred_element_type=F32)
            weight = jnp.exp2(score)
            t_ref[h * 8 : (h + 1) * 8, :] += jnp.sum(
                weight.reshape(sub // 8, 8, weight.shape[1]), axis=0
            )
            narrow = weight.astype(BF16)
            own = slice(h * depth, (h + 1) * depth)
            o_ref[own, :] += jnp.dot(
                vr[own], narrow * cos, preferred_element_type=F32
            ) + jnp.dot(vi[own], narrow * sin, preferred_element_type=F32)


def attend(lat, factor, key_scaled, value_scaled_t, queries, bias, cos, sin):
    heads, _, atoms = queries.shape
    width = value_scaled_t.shape[0]
    subs = lat.rows // SUB_ROWS
    per_step = max(n for n in (1, 2, 3, 4) if subs % n == 0)
    step = per_step * SUB_ROWS

    def whole(array):
        return pl.BlockSpec(array.shape, lambda i: (0,) * array.ndim)

    def rows(array):
        return pl.BlockSpec((step, array.shape[1]), lambda i: (i, 0))

    return pl.pallas_call(
        functools.partial(attend_kernel, heads),
        grid=(subs // per_step,),
        in_specs=[
            rows(factor),
            whole(key_scaled),
            whole(value_scaled_t),
            whole(queries),
            rows(bias),
            rows(cos),
            rows(sin),
        ],
        out_specs=[
            pl.BlockSpec((width, atoms), lambda i: (0, 0)),
            pl.BlockSpec((8 * heads, atoms), lambda i: (0, 0)),
        ],
        out_shape=[
            jax.ShapeDtypeStruct((width, atoms), F32),
            jax.ShapeDtypeStruct((8 * heads, atoms), F32),
        ],
        name="attend",
    )(factor, key_scaled, value_scaled_t, queries, bias, cos, sin)


def gather_blocks(block, axis):
    devices = lax.axis_size(axis)
    if devices & (devices - 1):
        return lax.all_gather(block, axis, axis=0)
    held = block[None]
    bit = devices // 2
    while bit:
        partners = [(i, i ^ bit) for i in range(devices)]
        held = jnp.concatenate([held, lax.ppermute(held, axis, partners)], axis=0)
        bit //= 2
    return held


def split_three(values):
    high = lax.reduce_precision(values, 8, 7)
    rest = values - high
    mid = lax.reduce_precision(rest, 8, 7)
    return jnp.concatenate([high, mid, rest - mid], axis=0).astype(BF16)


def rms_scale(values, axis):
    return values * lax.rsqrt(jnp.mean(values * values, axis=axis, keepdims=True) + EPS)


def body(
    features, species, positions, miller, species_table, w_query, w_key, w_value, w_out, temper
):
    lat = Lattice(miller.shape[1])
    local = features.shape[0]
    devices = lax.axis_size("atom")
    atoms = local * devices
    heads = temper.shape[1]
    key_width = w_query.shape[2]
    depth = key_width // heads
    channels = features.shape[1]
    levels = jnp.arange(species_table.shape[0], dtype=jnp.int32)
    onehot = (species[:, None] == levels[None, :]).astype(BF16)
    hidden = (
        features.astype(F32) + jnp.dot(onehot, species_table, preferred_element_type=F32)
    ).astype(BF16)

    pos_rows = split_three(positions).reshape(-1, channels)
    pad = -pos_rows.shape[0] % ROW_TILE
    first = gather_blocks(
        jnp.concatenate([hidden, pos_rows, jnp.zeros((pad, channels), BF16)], axis=0), "atom"
    )
    hidden_all = first[:, :local].reshape(atoms, channels)
    pieces = first[:, local : local + pos_rows.shape[0]].reshape(devices, 3, 3, local).astype(F32)
    pos_all = (pieces[:, 0] + pieces[:, 1] + pieces[:, 2]).transpose(1, 0, 2).reshape(3, atoms)

    pair_cols = jnp.asarray(np.stack([lat.px, lat.py], axis=1).astype(np.float32))
    cos, sin = local_tables(lat, pair_cols, positions)
    chunk = math.gcd(atoms, 1024)
    pair_cos, pair_sin = pair_tables(pair_cols, pos_all, chunk)
    z_turns = pos_all[2][:, None] * jnp.arange(16, dtype=F32)[None, :]
    z_cols = jnp.concatenate(cos_sin_turns(z_turns), axis=1)

    last = Lattice.code(miller[0, lat.inner :], miller[1, lat.inner :], miller[2, lat.inner :])

    def present(length, code):
        found = jnp.any(jnp.asarray(code)[..., None] == last, axis=-1)
        length = jnp.asarray(length)
        return (length < lat.radius) | ((length == lat.radius) & found)

    lengths = jnp.asarray(lat.tab_len).astype(F32)
    damp = jnp.where(
        present(lat.tab_len, lat.tab_code), jnp.exp(-DAMP * lengths) / math.sqrt(atoms), 0.0
    )
    lane = jnp.arange(128, dtype=jnp.int32)[None, :]
    absent = ~present(lat.row_len, lat.row_code)
    bias = jnp.where(absent[:, None] & (lane == 0), NEVER, 0.0).astype(BF16)
    head_of = jnp.arange(key_width, dtype=jnp.int32) // depth
    own_head = head_of[None, :] == jnp.arange(heads, dtype=jnp.int32)[:, None]
    bias_rows = jnp.zeros((heads, 128, local), F32).at[:, 0, :].set(1.0).astype(BF16)

    for layer in range(w_query.shape[0]):
        if layer:
            hidden_all = gather_blocks(hidden, "atom").reshape(atoms, channels)
        factor, squares = factors(lat, hidden_all, z_cols, pair_cos, pair_sin, damp)
        power = jnp.sum(squares, axis=0)
        power_scale = lax.rsqrt((power[:channels] + power[channels:]) / miller.shape[1] + POWER_EPS)
        both_scale = jnp.concatenate([power_scale, power_scale])
        key_scaled = (both_scale[:, None] * w_key[layer].astype(F32)).astype(BF16)
        value_scaled_t = (power_scale[:, None] * w_value[layer].astype(F32)).astype(BF16).T
        raw = jnp.dot(hidden, w_query[layer], preferred_element_type=F32)
        to_log2 = jnp.repeat(temper[layer] * (math.log2(math.e) / 16.0), depth)
        query_t = (rms_scale(raw, -1) * to_log2[None, :]).astype(BF16).T
        by_head = jnp.where(own_head[:, :, None], query_t[None], jnp.zeros((), BF16))
        queries = jnp.concatenate([by_head, bias_rows], axis=1)
        numerator, totals = attend(
            lat, factor, key_scaled, value_scaled_t, queries, bias, cos, sin
        )
        totals = jnp.sum(totals.reshape(heads, 8, local), axis=1)
        mixed = (numerator.reshape(heads, depth, local) / totals[:, None, :]).reshape(
            key_width, local
        )
        normed = rms_scale(mixed, 0).astype(BF16)
        hidden = (
            hidden.astype(F32)
            + lax.dot_general(normed, w_out[layer], (((0,), (0,)), ((), ())), preferred_element_type=F32)
        ).astype(BF16)
    return hidden


def solution(mesh):
    in_specs = (
        P(("group", "atom"), None),
        P(("group", "atom")),
        P(None, ("group", "atom")),
        P(),
        P(),
        P(),
        P(),
        P(),
        P(),
        P(),
    )
    out_specs = P(("group", "atom"), None)
    return jax.shard_map(body, mesh=mesh, in_specs=in_specs, out_specs=out_specs, check_vma=False)
```

```python
import functools
import math

import jax
import jax.numpy as jnp
import numpy as np
from jax import lax
from jax.experimental import pallas as pl
from jax.experimental.pallas import tpu as pltpu
from jax._src.pallas.mosaic.core import AccMemorySpace
from jax.sharding import PartitionSpec as P

DAMP = 0.005
EPS = 1e-06
POWER_EPS = 1e-05
MILLER_MAX = 13
ROW_TILE = 16
HALVES = 2
SUB_ROWS = 256
STEP_ROWS = 3 * SUB_ROWS
AHEAD = 2
NEVER = -30000.0
F32 = jnp.float32
BF16 = jnp.bfloat16
NT = (((1,), (1,)), ((), ()))


class Lattice:
    def __init__(self, kvecs):
        top = MILLER_MAX
        side = np.arange(-top, top + 1)
        gx, gy, gz = np.meshgrid(side, side, side, indexing="ij")
        upper = (gx > 0) | ((gx == 0) & (gy > 0)) | ((gx == 0) & (gy == 0) & (gz > 0))
        lengths = np.sort((gx * gx + gy * gy + gz * gz)[upper])
        self.radius = int(lengths[kvecs - 1])
        self.inner = int((lengths < self.radius).sum())
        pairs = [(x, y) for x in range(top + 1) for y in range(-top, top + 1) if x > 0 or y >= 0]
        pairs.sort(key=lambda p: p[0] ** 2 + p[1] ** 2)
        count = round_up(-(-len(pairs) // HALVES), ROW_TILE)
        self.pair_rows = count
        spread = np.zeros((2, HALVES * count), np.int32)
        spread[:, : len(pairs)] = np.array(pairs).T
        real = (np.arange(HALVES * count) < len(pairs)).reshape(count, HALVES).T
        px, py = spread.reshape(2, count, HALVES).transpose(0, 2, 1)
        self.pairs = np.stack([px, py], axis=2).astype(np.float32)
        flat = px**2 + py**2
        self.planes = []
        self.heights = []
        offset = 0
        self.levels = 2 * top + 1
        self.tab_len = np.full((HALVES, count, self.levels), self.radius + 1, np.int32)
        self.tab_code = np.full((HALVES, count, self.levels), -1, np.int32)
        for level in range(top + 1):
            inside = real & (flat + level * level <= self.radius)
            height = round_up(int(inside.sum(axis=1).max()), ROW_TILE)
            self.heights.append(height)
            offsets = []
            for sign in (1, -1) if level else (1,):
                mz = sign * level
                keep = inside & ((px > 0) | (py > 0) | (mz > 0))
                column = 2 * level - (1 if sign > 0 else 0) if level else 0
                self.tab_len[:, :, column] = np.where(keep, flat + mz * mz, self.radius + 1)
                self.tab_code[:, :, column] = np.where(keep, self.code(px, py, mz), -1)
                offsets.append((offset, column))
                offset += height
            self.planes.append(offsets)
        self.used = offset
        self.rows = round_up(offset, STEP_ROWS)

    @staticmethod
    def code(x, y, z):
        return ((x + 16) * 32 + (y + 16)) * 32 + (z + 16)


def round_up(value, step):
    return -(-value // step) * step


def fit_half_turn():
    nodes = 0.25 * (1 + np.cos(np.pi * (np.arange(64) + 0.5) / 64))
    square = nodes * nodes
    sine = np.polynomial.polynomial.polyfit(square, np.sin(np.pi * nodes) / nodes, 4)
    cosine = np.polynomial.polynomial.polyfit(square, np.cos(np.pi * nodes), 4)
    return [float(v) for v in sine], [float(v) for v in cosine]


SINE, COSINE = fit_half_turn()


def horner(coefs, u):
    total = jnp.full_like(u, coefs[-1])
    for c in coefs[-2::-1]:
        total = total * u + c
    return total


def cos_sin_turns(turns):
    part = turns - jnp.floor(turns + 0.5)
    u = part * part
    half_sin = part * horner(SINE, u)
    half_cos = horner(COSINE, u)
    return 1.0 - 2.0 * half_sin * half_sin, 2.0 * half_sin * half_cos


def vmem():
    return pl.BlockSpec(memory_space=pltpu.VMEM)


def pair_kernel(pair_ref, pos_ref, out_ref):
    turns = pair_ref[:, 0:1] * pos_ref[0:1, :] + pair_ref[:, 1:2] * pos_ref[1:2, :]
    c, s = cos_sin_turns(turns)
    for row in range(0, c.shape[0], ROW_TILE):
        out_ref[0, 2 * row : 2 * row + ROW_TILE, :] = c[row : row + ROW_TILE].astype(BF16)
        out_ref[0, 2 * row + ROW_TILE : 2 * row + 2 * ROW_TILE, :] = s[
            row : row + ROW_TILE
        ].astype(BF16)


def pair_tables(pair_cols, pos, chunk):
    rows, atoms = pair_cols.shape[0], pos.shape[1]
    out = jax.ShapeDtypeStruct((atoms // chunk, 2 * rows, chunk), BF16)
    return pl.pallas_call(
        pair_kernel,
        grid=(atoms // chunk,),
        in_specs=[
            pl.BlockSpec(pair_cols.shape, lambda i: (0, 0)),
            pl.BlockSpec((pos.shape[0], chunk), lambda i: (0, i)),
        ],
        out_specs=pl.BlockSpec((1, 2 * rows, chunk), lambda i: (i, 0, 0)),
        out_shape=out,
        name="pair_tables",
    )(pair_cols, pos)


def local_kernel(lat, pair_ref, pos_ref, damp_ref, cos_ref, sin_ref, bias_ref, c_buf, s_buf):
    turns = pair_ref[:, 0:1] * pos_ref[0:1, :] + pair_ref[:, 1:2] * pos_ref[1:2, :]
    c, s = cos_sin_turns(turns)
    c_buf[...] = c
    s_buf[...] = s
    lane = lax.broadcasted_iota(jnp.int32, (ROW_TILE, bias_ref.shape[1]), 1)
    turn_z = [cos_sin_turns(float(n) * pos_ref[2:3, :]) for n in range(len(lat.heights))]

    def tile(row, level):
        cz, sz = turn_z[level]
        for half in range(HALVES):
            own = pl.ds(half * lat.pair_rows + row, ROW_TILE)
            c1, s1 = c_buf[own, :], s_buf[own, :]
            cc, ss, sc, cs = c1 * cz, s1 * sz, s1 * cz, c1 * sz
            signed = ((cc - ss, sc + cs), (cc + ss, sc - cs))
            for (offset, column), values in zip(lat.planes[level], signed):
                to = pl.ds(half * lat.rows + offset + row, ROW_TILE)
                cos_ref[to, :] = values[0].astype(BF16)
                sin_ref[to, :] = values[1].astype(BF16)
                absent = damp_ref[own, column : column + 1] <= 0.0
                bias_ref[to, :] = jnp.where(absent & (lane == 0), NEVER, 0.0).astype(BF16)

    def common(index, carry):
        for level in range(len(lat.heights)):
            tile(pl.multiple_of(index * ROW_TILE, ROW_TILE), level)
        return carry

    shared = min(lat.heights) // ROW_TILE
    lax.fori_loop(0, shared, common, 0)
    for level, height in enumerate(lat.heights):
        for index in range(shared, height // ROW_TILE):
            tile(index * ROW_TILE, level)
    spare = lat.rows - lat.used
    if spare:
        for half in range(HALVES):
            to = pl.ds(half * lat.rows + lat.used, spare)
            cos_ref[to, :] = jnp.zeros((spare, cos_ref.shape[1]), BF16)
            sin_ref[to, :] = jnp.zeros((spare, sin_ref.shape[1]), BF16)
            first = lax.broadcasted_iota(jnp.int32, (spare, bias_ref.shape[1]), 1) == 0
            bias_ref[to, :] = jnp.where(first, NEVER, 0.0).astype(BF16)


def local_tables(lat, pair_cols, pos, damp):
    atoms = pos.shape[1]
    out = jax.ShapeDtypeStruct((HALVES * lat.rows, atoms), BF16)
    return pl.pallas_call(
        functools.partial(local_kernel, lat),
        in_specs=[vmem()] * 3,
        out_specs=[vmem()] * 3,
        out_shape=[out, out, jax.ShapeDtypeStruct((HALVES * lat.rows, 128), BF16)],
        scratch_shapes=[pltpu.VMEM((HALVES * lat.pair_rows, atoms), F32)] * 2,
        name="local_tables",
    )(pair_cols, pos, damp)


def factor_kernel(lat, h_ref, z_ref, pair_ref, damp_ref, f_ref, pow_ref, acc, turned):
    chunks, chunk, width = h_ref.shape
    total = jnp.zeros((8, 2 * width), F32)
    last = len(lat.heights) - 1
    for level, (height, offsets) in enumerate(zip(lat.heights, lat.planes)):
        reach = 2 * width if level else width
        acc[0 : 2 * height, :reach] = jnp.zeros((2 * height, reach), F32)
        cut = chunk // 2

        def step(index, carry):
            rhs = turned.at[level % 2, index] if level else h_ref.at[index]
            table = pair_ref.at[index]
            low = jnp.dot(table[: 2 * height, :cut], rhs[:cut, :], preferred_element_type=F32)
            high = jnp.dot(table[: 2 * height, cut:], rhs[cut:, :], preferred_element_type=F32)
            acc[0 : 2 * height, :reach] += low + high
            if level < last:
                h = h_ref[index]
                nxt, slot = level + 1, (level + 1) % 2
                turned[slot, index, :, :width] = h * z_ref[index, :, nxt : nxt + 1]
                turned[slot, index, :, width:] = h * z_ref[index, :, 16 + nxt : 17 + nxt]
            return carry

        lax.fori_loop(0, chunks, step, 0)
        both = acc[0 : 2 * height, :reach].reshape(-1, 2, ROW_TILE, reach)
        on_cos = both[:, 0].reshape(height, reach)
        on_sin = both[:, 1].reshape(height, reach)
        cc, sc = on_cos[:, :width], on_sin[:, :width]
        if level:
            cs, ss = on_cos[:, width:], on_sin[:, width:]
            signed = ((cc - ss, sc + cs), (cc + ss, sc - cs))
        else:
            signed = ((cc, sc),)
        for (offset, column), (real, imag) in zip(offsets, signed):
            damp = damp_ref[:height, column : column + 1]
            value = jnp.concatenate([real * damp, imag * damp], axis=1).astype(BF16)
            f_ref[offset : offset + height, :] = value
            wide = value.astype(F32)
            total = total + jnp.sum((wide * wide).reshape(height // 8, 8, 2 * width), axis=0)
    if lat.rows > lat.used:
        f_ref[lat.used :, :] = jnp.zeros((lat.rows - lat.used, 2 * width), BF16)
    pow_ref[...] = total


def factors(lat, hidden, z_cols, pair_rows, damp):
    chunks, _, chunk = pair_rows.shape
    width = hidden.shape[1]
    return pl.pallas_call(
        functools.partial(factor_kernel, lat),
        in_specs=[vmem()] * 4,
        out_specs=[vmem()] * 2,
        out_shape=[
            jax.ShapeDtypeStruct((lat.rows, 2 * width), BF16),
            jax.ShapeDtypeStruct((8, 2 * width), F32),
        ],
        scratch_shapes=[
            pltpu.VMEM((2 * lat.pair_rows, 2 * width), F32),
            pltpu.VMEM((2, chunks, chunk, 2 * width), BF16),
        ],
        name="factors",
    )(
        hidden.reshape(chunks, chunk, width),
        z_cols.reshape(chunks, chunk, z_cols.shape[1]),
        pair_rows,
        damp,
    )


def unit_accumulators(heads, depth, atoms):
    slots = range(AHEAD + 1)
    scores = [AccMemorySpace(m)((SUB_ROWS, atoms), F32) for m in range(2) for _ in slots]
    return scores + [AccMemorySpace(h % 2)((depth, atoms), F32) for h in range(heads)]


def attend_kernel(heads, *refs):
    depth, atoms = refs[7].shape[0] // heads, refs[7].shape[1]
    pl.run_scoped(
        functools.partial(attend_step, heads, refs), *unit_accumulators(heads, depth, atoms)
    )


def attend_step(heads, refs, *results):
    f_ref, b_ref, c_ref, s_ref, ks_ref, vs_ref, q_ref, o_ref, t_ref = refs
    keys, values = {}, {}
    slots = AHEAD + 1
    scores, gained = (results[:slots], results[slots : 2 * slots]), results[2 * slots :]
    depth, sub = o_ref.shape[0] // heads, SUB_ROWS
    subs = c_ref.shape[0] // sub
    projected = (scores[0][AHEAD], scores[1][AHEAD])

    def start_project(rows_ref, j):
        f = rows_ref[j * sub : (j + 1) * sub, :]
        pltpu.matmul_push_rhs(ks_ref[...], 0, 0)
        pltpu.matmul_acc_lhs(projected[0], f, load_staged_rhs=0)
        pltpu.matmul_push_rhs(f, 0, 1, transpose=True)
        pltpu.matmul_acc_lhs(projected[1], vs_ref[...], load_staged_rhs=0)

    def end_project(more_ref, j):
        key = pltpu.matmul_pop(projected[0])[:, : ks_ref.shape[1] // 2]
        key = (key * lax.rsqrt(jnp.mean(key * key, axis=-1, keepdims=True) + EPS)).astype(BF16)
        keys[j] = jnp.concatenate([key, more_ref[j * sub : (j + 1) * sub, :]], axis=1)
        values[j] = pltpu.matmul_pop(projected[1]).astype(BF16)

    @pl.when(pl.program_id(0) == 0)
    def _():
        o_ref[...] = jnp.zeros_like(o_ref)
        t_ref[...] = jnp.zeros_like(t_ref)

    for j in range(subs):
        start_project(f_ref, j)
        end_project(b_ref, j)

    units = [(j, h) for j in range(subs) for h in range(heads)]
    turns = {unit: (unit[1] // 2 + unit[0] * (heads // 2)) % AHEAD for unit in units}

    def issue(unit):
        j, h = unit
        pltpu.matmul_push_rhs(q_ref[h], 0, h % 2)
        pltpu.matmul_acc_lhs(scores[h % 2][turns[unit]], keys[j], load_staged_rhs=0)

    def finish(unit):
        j, h = unit
        span = slice(j * sub, (j + 1) * sub)
        weight = jnp.exp2(pltpu.matmul_pop(scores[h % 2][turns[unit]]))
        t_ref[h * 8 : (h + 1) * 8, :] += jnp.sum(
            weight.reshape(sub // 8, 8, weight.shape[1]), axis=0
        )
        narrow = weight.astype(BF16)
        half = values[j].shape[0] // 2
        for base, table in ((0, c_ref), (half, s_ref)):
            pltpu.matmul_push_rhs(narrow * table[span, :], 1, h % 2)
            rows = slice(base + h * depth, base + (h + 1) * depth)
            pltpu.matmul_acc_lhs(gained[h], values[j][rows, :], load_staged_rhs=1)

    lead = 2 * (AHEAD - 1)
    for unit in units[:lead]:
        issue(unit)
    for index, unit in enumerate(units):
        if index + lead < len(units):
            issue(units[index + lead])
        finish(unit)
    for h in range(heads):
        o_ref[h * depth : (h + 1) * depth, :] += pltpu.matmul_pop(gained[h])


def attend(lat, half, factor, key_scaled, value_scaled_t, queries, bias, cos, sin):
    heads, width, atoms = queries.shape
    step = STEP_ROWS
    steps = lat.rows // step
    first = half * steps

    def whole(array):
        return pl.BlockSpec(array.shape, lambda i: (0,) * array.ndim)

    def rows(array, skip):
        return pl.BlockSpec((step, array.shape[1]), lambda i: (i + skip, 0))

    key_width = width // 2
    empty = jnp.zeros_like(value_scaled_t)
    both_values = jnp.concatenate(
        [
            jnp.concatenate([value_scaled_t, empty], axis=1),
            jnp.concatenate([empty, value_scaled_t], axis=1),
        ],
        axis=0,
    )
    key_scaled = jnp.concatenate([key_scaled, jnp.zeros_like(key_scaled)], axis=1)
    return pl.pallas_call(
        functools.partial(attend_kernel, heads),
        grid=(steps,),
        in_specs=[
            rows(factor, 0),
            rows(bias, first),
            rows(cos, first),
            rows(sin, first),
            whole(key_scaled),
            whole(both_values),
            whole(queries),
        ],
        out_specs=[
            pl.BlockSpec((key_width, atoms), lambda i: (0, 0)),
            pl.BlockSpec((8 * heads, atoms), lambda i: (0, 0)),
        ],
        out_shape=[
            jax.ShapeDtypeStruct((key_width, atoms), F32),
            jax.ShapeDtypeStruct((8 * heads, atoms), F32),
        ],
        name="attend",
    )(factor, bias, cos, sin, key_scaled, both_values, queries)


def gather_blocks(block, axis):
    devices = lax.axis_size(axis)
    if devices & (devices - 1):
        return lax.all_gather(block, axis, axis=0)
    held = block[None]
    bit = devices // 2
    while bit:
        partners = [(i, i ^ bit) for i in range(devices)]
        held = jnp.concatenate([held, lax.ppermute(held, axis, partners)], axis=0)
        bit //= 2
    return held


def split_three(values):
    high = lax.reduce_precision(values, 8, 7)
    rest = values - high
    mid = lax.reduce_precision(rest, 8, 7)
    return jnp.concatenate([high, mid, rest - mid], axis=0).astype(BF16)


def rms_scale(values, axis):
    return values * lax.rsqrt(jnp.mean(values * values, axis=axis, keepdims=True) + EPS)


def body(
    features, species, positions, miller, species_table, w_query, w_key, w_value, w_out, temper
):
    lat = Lattice(miller.shape[1])
    local = features.shape[0]
    devices = lax.axis_size("atom")
    atoms = local * devices
    heads = temper.shape[1]
    key_width = w_query.shape[2]
    depth = key_width // heads
    channels = features.shape[1]
    levels = jnp.arange(species_table.shape[0], dtype=jnp.int32)
    onehot = (species[:, None] == levels[None, :]).astype(BF16)
    hidden = (
        features.astype(F32) + jnp.dot(onehot, species_table, preferred_element_type=F32)
    ).astype(BF16)

    pos_rows = split_three(positions).reshape(-1, channels)
    pad = -pos_rows.shape[0] % ROW_TILE
    first = gather_blocks(
        jnp.concatenate([hidden, pos_rows, jnp.zeros((pad, channels), BF16)], axis=0), "atom"
    )
    hidden_all = first[:, :local].reshape(atoms, channels)
    pieces = first[:, local : local + pos_rows.shape[0]].reshape(devices, 3, 3, local).astype(F32)
    pos_all = (pieces[:, 0] + pieces[:, 1] + pieces[:, 2]).transpose(1, 0, 2).reshape(3, atoms)

    other = lax.axis_index("atom") % HALVES == 1

    def own_first(table):
        return jnp.where(other, jnp.asarray(table[::-1].copy()), jnp.asarray(table)).reshape(
            HALVES * lat.pair_rows, table.shape[2]
        )

    last = Lattice.code(miller[0, lat.inner :], miller[1, lat.inner :], miller[2, lat.inner :])
    lengths, codes = own_first(lat.tab_len), own_first(lat.tab_code)
    found = jnp.any(codes[:, :, None] == last, axis=-1)
    present = (lengths < lat.radius) | ((lengths == lat.radius) & found)
    damp = jnp.where(present, jnp.exp(-DAMP * lengths.astype(F32)) / math.sqrt(atoms), 0.0)
    pair_cols = own_first(lat.pairs)
    cos, sin, bias = local_tables(lat, pair_cols, positions, damp)
    chunk = math.gcd(atoms, 1024)
    own_damp = damp[: lat.pair_rows]
    pair_rows = pair_tables(pair_cols[: lat.pair_rows], pos_all, chunk)
    z_turns = pos_all[2][:, None] * jnp.arange(16, dtype=F32)[None, :]
    z_cols = jnp.concatenate(cos_sin_turns(z_turns), axis=1).astype(BF16)
    head_of = jnp.arange(key_width, dtype=jnp.int32) // depth
    own_head = head_of[None, :] == jnp.arange(heads, dtype=jnp.int32)[:, None]
    bias_rows = jnp.zeros((heads, 128, local), F32).at[:, 0, :].set(1.0).astype(BF16)

    for layer in range(w_query.shape[0]):
        if layer:
            hidden_all = gather_blocks(hidden, "atom").reshape(atoms, channels)
        factor, squares = factors(lat, hidden_all, z_cols, pair_rows, own_damp)
        squares = jnp.sum(squares, axis=0, keepdims=True)
        swap = [(i, i ^ 1) for i in range(devices)]
        power = (squares + lax.ppermute(squares, "atom", swap))[0]
        theirs = lax.ppermute(factor, "atom", swap)
        power_scale = lax.rsqrt((power[:channels] + power[channels:]) / miller.shape[1] + POWER_EPS)
        both_scale = jnp.concatenate([power_scale, power_scale])
        key_scaled = (both_scale[:, None] * w_key[layer].astype(F32)).astype(BF16)
        value_scaled_t = (power_scale[:, None] * w_value[layer].astype(F32)).astype(BF16).T
        raw = jnp.dot(hidden, w_query[layer], preferred_element_type=F32)
        to_log2 = jnp.repeat(temper[layer] * (math.log2(math.e) / 16.0), depth)
        query_t = (rms_scale(raw, -1) * to_log2[None, :]).astype(BF16).T
        by_head = jnp.where(own_head[:, :, None], query_t[None], jnp.zeros((), BF16))
        queries = jnp.concatenate([by_head, bias_rows], axis=1)
        numerator, totals = 0.0, 0.0
        for half, rows in enumerate((factor, theirs)):
            gained, weight = attend(
                lat, half, rows, key_scaled, value_scaled_t, queries, bias, cos, sin
            )
            numerator, totals = numerator + gained, totals + weight
        totals = jnp.sum(totals.reshape(heads, 8, local), axis=1)
        mixed = (numerator.reshape(heads, depth, local) / totals[:, None, :]).reshape(
            key_width, local
        )
        normed = rms_scale(mixed, 0).astype(BF16)
        hidden = (
            hidden.astype(F32)
            + lax.dot_general(normed, w_out[layer], (((0,), (0,)), ((), ())), preferred_element_type=F32)
        ).astype(BF16)
    return hidden


def solution(mesh):
    in_specs = (
        P(("group", "atom"), None),
        P(("group", "atom")),
        P(None, ("group", "atom")),
        P(),
        P(),
        P(),
        P(),
        P(),
        P(),
        P(),
    )
    out_specs = P(("group", "atom"), None)
    return jax.shard_map(body, mesh=mesh, in_specs=in_specs, out_specs=out_specs, check_vma=False)
```

```python
import functools
import math

import jax
import jax.numpy as jnp
import numpy as np
from jax import lax
from jax.experimental import pallas as pl
from jax.experimental.pallas import tpu as pltpu
from jax._src.pallas.mosaic.core import AccMemorySpace
from jax.sharding import PartitionSpec as P

DAMP = 0.005
EPS = 1e-06
POWER_EPS = 1e-05
MILLER_MAX = 13
ROW_TILE = 16
HALVES = 2
SUB_ROWS = 256
STEP_ROWS = 3 * SUB_ROWS
AHEAD = 2
NEVER = -30000.0
F32 = jnp.float32
BF16 = jnp.bfloat16
NT = (((1,), (1,)), ((), ()))


class Lattice:
    def __init__(self, kvecs):
        top = MILLER_MAX
        side = np.arange(-top, top + 1)
        gx, gy, gz = np.meshgrid(side, side, side, indexing="ij")
        upper = (gx > 0) | ((gx == 0) & (gy > 0)) | ((gx == 0) & (gy == 0) & (gz > 0))
        lengths = np.sort((gx * gx + gy * gy + gz * gz)[upper])
        self.radius = int(lengths[kvecs - 1])
        self.inner = int((lengths < self.radius).sum())
        pairs = [(x, y) for x in range(top + 1) for y in range(-top, top + 1) if x > 0 or y >= 0]
        pairs.sort(key=lambda p: p[0] ** 2 + p[1] ** 2)
        count = round_up(-(-len(pairs) // HALVES), ROW_TILE)
        self.pair_rows = count
        spread = np.zeros((2, HALVES * count), np.int32)
        spread[:, : len(pairs)] = np.array(pairs).T
        real = (np.arange(HALVES * count) < len(pairs)).reshape(count, HALVES).T
        px, py = spread.reshape(2, count, HALVES).transpose(0, 2, 1)
        self.pairs = np.stack([px, py], axis=2).astype(np.float32)
        flat = px**2 + py**2
        self.planes = []
        self.heights = []
        offset = 0
        self.levels = 2 * top + 1
        self.tab_len = np.full((HALVES, count, self.levels), self.radius + 1, np.int32)
        self.tab_code = np.full((HALVES, count, self.levels), -1, np.int32)
        for level in range(top + 1):
            inside = real & (flat + level * level <= self.radius)
            height = round_up(int(inside.sum(axis=1).max()), ROW_TILE)
            self.heights.append(height)
            offsets = []
            for sign in (1, -1) if level else (1,):
                mz = sign * level
                keep = inside & ((px > 0) | (py > 0) | (mz > 0))
                column = 2 * level - (1 if sign > 0 else 0) if level else 0
                self.tab_len[:, :, column] = np.where(keep, flat + mz * mz, self.radius + 1)
                self.tab_code[:, :, column] = np.where(keep, self.code(px, py, mz), -1)
                offsets.append((offset, column))
                offset += height
            self.planes.append(offsets)
        self.used = offset
        self.rows = round_up(offset, STEP_ROWS)

    @staticmethod
    def code(x, y, z):
        return ((x + 16) * 32 + (y + 16)) * 32 + (z + 16)


def round_up(value, step):
    return -(-value // step) * step


def fit_half_turn():
    nodes = 0.25 * (1 + np.cos(np.pi * (np.arange(64) + 0.5) / 64))
    square = nodes * nodes
    sine = np.polynomial.polynomial.polyfit(square, np.sin(np.pi * nodes) / nodes, 4)
    cosine = np.polynomial.polynomial.polyfit(square, np.cos(np.pi * nodes), 4)
    return [float(v) for v in sine], [float(v) for v in cosine]


SINE, COSINE = fit_half_turn()


def horner(coefs, u):
    total = jnp.full_like(u, coefs[-1])
    for c in coefs[-2::-1]:
        total = total * u + c
    return total


def cos_sin_turns(turns):
    part = turns - jnp.floor(turns + 0.5)
    u = part * part
    half_sin = part * horner(SINE, u)
    half_cos = horner(COSINE, u)
    return 1.0 - 2.0 * half_sin * half_sin, 2.0 * half_sin * half_cos


def vmem():
    return pl.BlockSpec(memory_space=pltpu.VMEM)


def pair_kernel(pair_ref, pos_ref, out_ref):
    turns = pair_ref[:, 0:1] * pos_ref[0:1, :] + pair_ref[:, 1:2] * pos_ref[1:2, :]
    c, s = cos_sin_turns(turns)
    for row in range(0, c.shape[0], ROW_TILE):
        out_ref[0, 2 * row : 2 * row + ROW_TILE, :] = c[row : row + ROW_TILE].astype(BF16)
        out_ref[0, 2 * row + ROW_TILE : 2 * row + 2 * ROW_TILE, :] = s[
            row : row + ROW_TILE
        ].astype(BF16)


def pair_tables(pair_cols, pos, chunk):
    rows, atoms = pair_cols.shape[0], pos.shape[1]
    out = jax.ShapeDtypeStruct((atoms // chunk, 2 * rows, chunk), BF16)
    return pl.pallas_call(
        pair_kernel,
        grid=(atoms // chunk,),
        in_specs=[
            pl.BlockSpec(pair_cols.shape, lambda i: (0, 0)),
            pl.BlockSpec((pos.shape[0], chunk), lambda i: (0, i)),
        ],
        out_specs=pl.BlockSpec((1, 2 * rows, chunk), lambda i: (i, 0, 0)),
        out_shape=out,
        name="pair_tables",
    )(pair_cols, pos)


def local_kernel(lat, pair_ref, pos_ref, damp_ref, cos_ref, sin_ref, bias_ref, c_buf, s_buf):
    turns = pair_ref[:, 0:1] * pos_ref[0:1, :] + pair_ref[:, 1:2] * pos_ref[1:2, :]
    c, s = cos_sin_turns(turns)
    c_buf[...] = c
    s_buf[...] = s
    lane = lax.broadcasted_iota(jnp.int32, (ROW_TILE, bias_ref.shape[1]), 1)
    turn_z = [cos_sin_turns(float(n) * pos_ref[2:3, :]) for n in range(len(lat.heights))]

    def tile(row, level):
        cz, sz = turn_z[level]
        for half in range(HALVES):
            own = pl.ds(half * lat.pair_rows + row, ROW_TILE)
            c1, s1 = c_buf[own, :], s_buf[own, :]
            cc, ss, sc, cs = c1 * cz, s1 * sz, s1 * cz, c1 * sz
            signed = ((cc - ss, sc + cs), (cc + ss, sc - cs))
            for (offset, column), values in zip(lat.planes[level], signed):
                to = pl.ds(half * lat.rows + offset + row, ROW_TILE)
                cos_ref[to, :] = values[0].astype(BF16)
                sin_ref[to, :] = values[1].astype(BF16)
                absent = damp_ref[own, column : column + 1] <= 0.0
                bias_ref[to, :] = jnp.where(absent & (lane == 0), NEVER, 0.0).astype(BF16)

    def common(index, carry):
        for level in range(len(lat.heights)):
            tile(pl.multiple_of(index * ROW_TILE, ROW_TILE), level)
        return carry

    shared = min(lat.heights) // ROW_TILE
    lax.fori_loop(0, shared, common, 0)
    for level, height in enumerate(lat.heights):
        for index in range(shared, height // ROW_TILE):
            tile(index * ROW_TILE, level)
    spare = lat.rows - lat.used
    if spare:
        for half in range(HALVES):
            to = pl.ds(half * lat.rows + lat.used, spare)
            cos_ref[to, :] = jnp.zeros((spare, cos_ref.shape[1]), BF16)
            sin_ref[to, :] = jnp.zeros((spare, sin_ref.shape[1]), BF16)
            first = lax.broadcasted_iota(jnp.int32, (spare, bias_ref.shape[1]), 1) == 0
            bias_ref[to, :] = jnp.where(first, NEVER, 0.0).astype(BF16)


def local_tables(lat, pair_cols, pos, damp):
    atoms = pos.shape[1]
    out = jax.ShapeDtypeStruct((HALVES * lat.rows, atoms), BF16)
    return pl.pallas_call(
        functools.partial(local_kernel, lat),
        in_specs=[vmem()] * 3,
        out_specs=[vmem()] * 3,
        out_shape=[out, out, jax.ShapeDtypeStruct((HALVES * lat.rows, 128), BF16)],
        scratch_shapes=[pltpu.VMEM((HALVES * lat.pair_rows, atoms), F32)] * 2,
        name="local_tables",
    )(pair_cols, pos, damp)


def factor_kernel(lat, h_ref, z_ref, pair_ref, damp_ref, f_ref, pow_ref, acc, turned):
    chunks, chunk, width = h_ref.shape
    total = jnp.zeros((8, 2 * width), F32)
    last = len(lat.heights) - 1
    for level, (height, offsets) in enumerate(zip(lat.heights, lat.planes)):
        reach = 2 * width if level else width
        acc[0 : 2 * height, :reach] = jnp.zeros((2 * height, reach), F32)
        cut = chunk // 2

        def step(index, carry):
            rhs = turned.at[level % 2, index] if level else h_ref.at[index]
            table = pair_ref.at[index]
            low = jnp.dot(table[: 2 * height, :cut], rhs[:cut, :], preferred_element_type=F32)
            high = jnp.dot(table[: 2 * height, cut:], rhs[cut:, :], preferred_element_type=F32)
            acc[0 : 2 * height, :reach] += low + high
            if level < last:
                h = h_ref[index]
                nxt, slot = level + 1, (level + 1) % 2
                turned[slot, index, :, :width] = h * z_ref[index, :, nxt : nxt + 1]
                turned[slot, index, :, width:] = h * z_ref[index, :, 16 + nxt : 17 + nxt]
            return carry

        lax.fori_loop(0, chunks, step, 0)
        both = acc[0 : 2 * height, :reach].reshape(-1, 2, ROW_TILE, reach)
        on_cos = both[:, 0].reshape(height, reach)
        on_sin = both[:, 1].reshape(height, reach)
        cc, sc = on_cos[:, :width], on_sin[:, :width]
        if level:
            cs, ss = on_cos[:, width:], on_sin[:, width:]
            signed = ((cc - ss, sc + cs), (cc + ss, sc - cs))
        else:
            signed = ((cc, sc),)
        for (offset, column), (real, imag) in zip(offsets, signed):
            damp = damp_ref[:height, column : column + 1]
            value = jnp.concatenate([real * damp, imag * damp], axis=1).astype(BF16)
            f_ref[offset : offset + height, :] = value
            wide = value.astype(F32)
            total = total + jnp.sum((wide * wide).reshape(height // 8, 8, 2 * width), axis=0)
    if lat.rows > lat.used:
        f_ref[lat.used :, :] = jnp.zeros((lat.rows - lat.used, 2 * width), BF16)
    pow_ref[...] = total


def factors(lat, hidden, z_cols, pair_rows, damp):
    chunks, _, chunk = pair_rows.shape
    width = hidden.shape[1]
    return pl.pallas_call(
        functools.partial(factor_kernel, lat),
        in_specs=[vmem()] * 4,
        out_specs=[vmem()] * 2,
        out_shape=[
            jax.ShapeDtypeStruct((lat.rows, 2 * width), BF16),
            jax.ShapeDtypeStruct((8, 2 * width), F32),
        ],
        scratch_shapes=[
            pltpu.VMEM((2 * lat.pair_rows, 2 * width), F32),
            pltpu.VMEM((2, chunks, chunk, 2 * width), BF16),
        ],
        name="factors",
    )(
        hidden.reshape(chunks, chunk, width),
        z_cols.reshape(chunks, chunk, z_cols.shape[1]),
        pair_rows,
        damp,
    )


def unit_accumulators(heads, depth, atoms):
    slots = range(AHEAD + 1)
    scores = [AccMemorySpace(m)((SUB_ROWS, atoms), F32) for m in range(2) for _ in slots]
    return scores + [AccMemorySpace(h % 2)((depth, atoms), F32) for h in range(heads)]


def attend_kernel(heads, *refs):
    depth, atoms = refs[7].shape[0] // heads, refs[7].shape[1]
    pl.run_scoped(
        functools.partial(attend_step, heads, refs), *unit_accumulators(heads, depth, atoms)
    )


def attend_step(heads, refs, *results):
    f_ref, b_ref, c_ref, s_ref, ks_ref, vs_ref, q_ref, o_ref, t_ref = refs
    keys, values = {}, {}
    slots = AHEAD + 1
    scores, gained = (results[:slots], results[slots : 2 * slots]), results[2 * slots :]
    depth, sub = o_ref.shape[0] // heads, SUB_ROWS
    subs = c_ref.shape[0] // sub
    projected = (scores[0][-1], scores[1][-1])

    def start_project(rows_ref, j):
        f = rows_ref[j * sub : (j + 1) * sub, :]
        pltpu.matmul_push_rhs(ks_ref[...], 0, 0)
        pltpu.matmul_acc_lhs(projected[0], f, load_staged_rhs=0)
        pltpu.matmul_push_rhs(f, 0, 1, transpose=True)
        pltpu.matmul_acc_lhs(projected[1], vs_ref[...], load_staged_rhs=0)

    def end_project(more_ref, j):
        key = pltpu.matmul_pop(projected[0])[:, : ks_ref.shape[1] // 2]
        key = (key * lax.rsqrt(jnp.mean(key * key, axis=-1, keepdims=True) + EPS)).astype(BF16)
        keys[j] = jnp.concatenate([key, more_ref[j * sub : (j + 1) * sub, :]], axis=1)
        values[j] = pltpu.matmul_pop(projected[1]).astype(BF16)

    @pl.when(pl.program_id(0) == 0)
    def _():
        o_ref[...] = jnp.zeros_like(o_ref)
        t_ref[...] = jnp.zeros_like(t_ref)

    for j in range(subs):
        start_project(f_ref, j)
        end_project(b_ref, j)

    units = [(j, h) for j in range(subs) for h in range(heads)]
    turns = {unit: (unit[1] // 2 + unit[0] * (heads // 2)) % AHEAD for unit in units}

    def issue(unit):
        j, h = unit
        pltpu.matmul_push_rhs(q_ref[h], 0, h % 2)
        pltpu.matmul_acc_lhs(scores[h % 2][turns[unit]], keys[j], load_staged_rhs=0)

    def finish(unit):
        j, h = unit
        span = slice(j * sub, (j + 1) * sub)
        weight = jnp.exp2(pltpu.matmul_pop(scores[h % 2][turns[unit]]))
        t_ref[h * 8 : (h + 1) * 8, :] += jnp.sum(
            weight.reshape(sub // 8, 8, weight.shape[1]), axis=0
        )
        narrow = weight.astype(BF16)
        half = values[j].shape[0] // 2
        for base, table in ((0, c_ref), (half, s_ref)):
            pltpu.matmul_push_rhs(narrow * table[span, :], 1, h % 2)
            rows = slice(base + h * depth, base + (h + 1) * depth)
            pltpu.matmul_acc_lhs(gained[h], values[j][rows, :], load_staged_rhs=1)

    lead = 2 * (AHEAD - 1)
    for unit in units[:lead]:
        issue(unit)
    for index, unit in enumerate(units):
        if index + lead < len(units):
            issue(units[index + lead])
        finish(unit)
    for h in range(heads):
        o_ref[h * depth : (h + 1) * depth, :] += pltpu.matmul_pop(gained[h])


def attend(lat, half, factor, key_scaled, value_scaled_t, queries, bias, cos, sin):
    heads, width, atoms = queries.shape
    step = STEP_ROWS
    steps = lat.rows // step
    first = half * steps

    def whole(array):
        return pl.BlockSpec(array.shape, lambda i: (0,) * array.ndim)

    def rows(array, skip):
        return pl.BlockSpec((step, array.shape[1]), lambda i: (i + skip, 0))

    key_width = width // 2
    empty = jnp.zeros_like(value_scaled_t)
    both_values = jnp.concatenate(
        [
            jnp.concatenate([value_scaled_t, empty], axis=1),
            jnp.concatenate([empty, value_scaled_t], axis=1),
        ],
        axis=0,
    )
    key_scaled = jnp.concatenate([key_scaled, jnp.zeros_like(key_scaled)], axis=1)
    return pl.pallas_call(
        functools.partial(attend_kernel, heads),
        grid=(steps,),
        in_specs=[
            rows(factor, 0),
            rows(bias, first),
            rows(cos, first),
            rows(sin, first),
            whole(key_scaled),
            whole(both_values),
            whole(queries),
        ],
        out_specs=[
            pl.BlockSpec((key_width, atoms), lambda i: (0, 0)),
            pl.BlockSpec((8 * heads, atoms), lambda i: (0, 0)),
        ],
        out_shape=[
            jax.ShapeDtypeStruct((key_width, atoms), F32),
            jax.ShapeDtypeStruct((8 * heads, atoms), F32),
        ],
        name="attend",
    )(factor, bias, cos, sin, key_scaled, both_values, queries)


def gather_blocks(block, axis, beside=()):
    devices = lax.axis_size(axis)
    if devices & (devices - 1):
        return lax.all_gather(block, axis, axis=0), beside
    held = block[None]
    bit = devices // 2
    while bit:
        if bit == 1 and beside:
            held, beside = lax.optimization_barrier((held, beside))
        partners = [(i, i ^ bit) for i in range(devices)]
        held = jnp.concatenate([held, lax.ppermute(held, axis, partners)], axis=0)
        bit //= 2
    return held, beside


def split_three(values):
    high = lax.reduce_precision(values, 8, 7)
    rest = values - high
    mid = lax.reduce_precision(rest, 8, 7)
    return jnp.concatenate([high, mid, rest - mid], axis=0).astype(BF16)


def rms_scale(values, axis):
    return values * lax.rsqrt(jnp.mean(values * values, axis=axis, keepdims=True) + EPS)


def body(
    features, species, positions, miller, species_table, w_query, w_key, w_value, w_out, temper
):
    lat = Lattice(miller.shape[1])
    local = features.shape[0]
    devices = lax.axis_size("atom")
    atoms = local * devices
    heads = temper.shape[1]
    key_width = w_query.shape[2]
    depth = key_width // heads
    channels = features.shape[1]
    levels = jnp.arange(species_table.shape[0], dtype=jnp.int32)
    onehot = (species[:, None] == levels[None, :]).astype(BF16)
    hidden = (
        features.astype(F32) + jnp.dot(onehot, species_table, preferred_element_type=F32)
    ).astype(BF16)

    other = lax.axis_index("atom") % HALVES == 1

    def own_first(table):
        return jnp.where(other, jnp.asarray(table[::-1].copy()), jnp.asarray(table)).reshape(
            HALVES * lat.pair_rows, table.shape[2]
        )

    last = Lattice.code(miller[0, lat.inner :], miller[1, lat.inner :], miller[2, lat.inner :])
    lengths, codes = own_first(lat.tab_len), own_first(lat.tab_code)
    found = jnp.any(codes[:, :, None] == last, axis=-1)
    present = (lengths < lat.radius) | ((lengths == lat.radius) & found)
    damp = jnp.where(present, jnp.exp(-DAMP * lengths.astype(F32)) / math.sqrt(atoms), 0.0)
    pair_cols = own_first(lat.pairs)
    cos, sin, bias = local_tables(lat, pair_cols, positions, damp)
    pos_rows = split_three(positions).reshape(-1, channels)
    pad = -pos_rows.shape[0] % ROW_TILE
    block = jnp.concatenate([hidden, pos_rows, jnp.zeros((pad, channels), BF16)], axis=0)
    first, (cos, sin, bias) = gather_blocks(block, "atom", (cos, sin, bias))
    hidden_all = first[:, :local].reshape(atoms, channels)
    pieces = first[:, local : local + pos_rows.shape[0]].reshape(devices, 3, 3, local).astype(F32)
    pos_all = (pieces[:, 0] + pieces[:, 1] + pieces[:, 2]).transpose(1, 0, 2).reshape(3, atoms)
    chunk = math.gcd(atoms, 1024)
    own_damp = damp[: lat.pair_rows]
    pair_rows = pair_tables(pair_cols[: lat.pair_rows], pos_all, chunk)
    z_turns = pos_all[2][:, None] * jnp.arange(16, dtype=F32)[None, :]
    z_cols = jnp.concatenate(cos_sin_turns(z_turns), axis=1).astype(BF16)
    head_of = jnp.arange(key_width, dtype=jnp.int32) // depth
    own_head = head_of[None, :] == jnp.arange(heads, dtype=jnp.int32)[:, None]
    bias_rows = jnp.zeros((heads, 128, local), F32).at[:, 0, :].set(1.0).astype(BF16)

    for layer in range(w_query.shape[0]):
        if layer:
            hidden_all = gather_blocks(hidden, "atom")[0].reshape(atoms, channels)
        factor, squares = factors(lat, hidden_all, z_cols, pair_rows, own_damp)
        squares = jnp.sum(squares, axis=0, keepdims=True)
        swap = [(i, i ^ 1) for i in range(devices)]
        power = (squares + lax.ppermute(squares, "atom", swap))[0]
        theirs = lax.ppermute(factor, "atom", swap)
        power_scale = lax.rsqrt((power[:channels] + power[channels:]) / miller.shape[1] + POWER_EPS)
        both_scale = jnp.concatenate([power_scale, power_scale])
        key_scaled = (both_scale[:, None] * w_key[layer].astype(F32)).astype(BF16)
        value_scaled_t = (power_scale[:, None] * w_value[layer].astype(F32)).astype(BF16).T
        raw = jnp.dot(hidden, w_query[layer], preferred_element_type=F32)
        to_log2 = jnp.repeat(temper[layer] * (math.log2(math.e) / 16.0), depth)
        query_t = (rms_scale(raw, -1) * to_log2[None, :]).astype(BF16).T
        by_head = jnp.where(own_head[:, :, None], query_t[None], jnp.zeros((), BF16))
        queries = jnp.concatenate([by_head, bias_rows], axis=1)
        numerator, totals = 0.0, 0.0
        for half, rows in enumerate((factor, theirs)):
            gained, weight = attend(
                lat, half, rows, key_scaled, value_scaled_t, queries, bias, cos, sin
            )
            numerator, totals = numerator + gained, totals + weight
        totals = jnp.sum(totals.reshape(heads, 8, local), axis=1)
        mixed = (numerator.reshape(heads, depth, local) / totals[:, None, :]).reshape(
            key_width, local
        )
        normed = rms_scale(mixed, 0).astype(BF16)
        hidden = (
            hidden.astype(F32)
            + lax.dot_general(normed, w_out[layer], (((0,), (0,)), ((), ())), preferred_element_type=F32)
        ).astype(BF16)
    return hidden


def solution(mesh):
    in_specs = (
        P(("group", "atom"), None),
        P(("group", "atom")),
        P(None, ("group", "atom")),
        P(),
        P(),
        P(),
        P(),
        P(),
        P(),
        P(),
    )
    out_specs = P(("group", "atom"), None)
    return jax.shard_map(body, mesh=mesh, in_specs=in_specs, out_specs=out_specs, check_vma=False)
```
